32 devices in a mesh: view: 4 (over y, core), bx: 2 (over x), by: 4 (over z).
Axes of the slice: x: 2, y: 2, z: 4, core: 2. Of those that a mesh axis runs over, the one named last changes fastest.
Arguments:
- estimate: float32 [2048, 512], P(('bx', 'by')), may hold values from 0.5 to 2
- recorded: float32 [4, 2048, 512], P('view', ('bx', 'by')), may hold values from 0.5 to 4
- resample: float32 [4, 4, 512, 512], P('view'), may hold values from 0 to 1, as said below
- psf_taps: float32 [4, 31], P('view'), may hold values from 0.2 to 1
- source_brick: int32 [4, 2048, 4], P('view', ('bx', 'by')), may hold values from 0 to 7, all different within a row; in each aligned block of 256 rows (0 to 255, 256 to 511, ..., all dimensions but the last counted through in order) at most 192 rows name the same one
- source_column: int32 [4, 2048, 4], P('view', ('bx', 'by')), may hold values from 0 to 255
Outputs:
- refined: float32 [2048, 512], P(('bx', 'by'))
The draws below stay inside these ranges and needn't reach their ends.
Inputs may be any that keep to these rules, and one draw needn't show every extreme that they name: `source_brick`: in each view, the 4 bricks named for one column are different; among the columns of one brick, no joined brick is named more than 192 times, and some joined brick exactly 192 times. `resample`: all entries are nonnegative.
All inputs are finite; a program needn't handle non-finite values.
Results may differ from the reference program's by a relative error of at most 0.0001.
Values sent between devices are 32-bit elements; how exact they have to be, the bound alone decides.
A program may use at most 192 MiB of HBM per device.

```python
import math
import jax
import jax.numpy as jnp
import numpy as np
from jax import lax

DEPTH = 512
COLUMNS = 256
SOURCES = 4
TAPS = 31
ITERS = 2
VIEWS = 4
BRICKS = 8
ALL_COLUMNS = 2048
CAPACITY = 192


def draw_resample(key, part):
    key_diag = jax.random.fold_in(key, 11)
    key_off = jax.random.fold_in(key, 12)
    diagonal = jax.random.uniform(key_diag, (VIEWS, SOURCES, DEPTH), jnp.float32, 0.05, 0.35)
    spread = jax.random.uniform(key_off, (VIEWS, SOURCES, DEPTH, DEPTH), jnp.float32) * (0.1 / DEPTH)
    identity = jnp.eye(DEPTH, dtype=jnp.float32)
    return spread + identity * diagonal[..., None]


def set_ends(drawn, own_key, least, high):
    extent = drawn.shape
    place = [jax.random.randint(jax.random.fold_in(own_key, axis), (), 0, extent[axis]) for axis in range(len(extent))]
    drawn = drawn.at[tuple(place)].set(least)
    longest = extent.index(max(extent))
    place[longest] = (place[longest] + 1) % extent[longest]
    return drawn.at[tuple(place)].set(high)


def levels(stream_key, shape, split, least, largest):
    factor_of, own = 1.0, jax.random.fold_in(stream_key, 6)
    for position, blocks in split:
        steps = jnp.exp(jax.random.uniform(jax.random.fold_in(own, position), (blocks,), jnp.float32, least / len(split), largest / len(split)))
        factor_of = factor_of * jnp.repeat(steps, shape[position] // blocks).reshape([-1 if axis == position else 1 for axis in range(len(shape))])
    return factor_of


def routed_block(key, own, number, rows, number_of, top, limit, skew):
    order = jax.random.permutation(key, number_of)
    crowded, common = portions_of(number_of, rows * top, limit, skew, True), portions_of(number_of, rows * top, limit, skew, False)
    places = jnp.arange(number_of)

    def named(sizes, turn):
        used = int((sizes > 0).sum())
        fixed = max(1, used // 4)
        shifted = fixed + (places - fixed + turn * (used - fixed)) % max(1, number_of - fixed)
        return jnp.zeros((number_of,), jnp.int32).at[order[jnp.where(places < fixed, places, shifted)]].set(jnp.asarray(sizes, jnp.int32))

    sizes = jnp.where(number % 4 == 0, named(crowded, number // 4), named(common, number - number // 4 - 1))
    mixed = jax.random.permutation(jax.random.fold_in(own, 3), number_of)
    giver, taker = mixed[0:number_of // 2 * 2:2], mixed[1:number_of // 2 * 2:2]
    slack = jnp.minimum(sizes[giver] - 1, limit - sizes[taker]) // 2
    slack = jnp.where((giver == order[0]) | (taker == order[0]) | (sizes[taker] == 0), 0, jnp.maximum(slack, 0))
    shifted = jax.random.randint(jax.random.fold_in(own, 4), (number_of // 2,), 0, 1 << 20) % (slack + 1)
    sizes = sizes.at[giver].add(-shifted).at[taker].add(shifted)
    labels = jnp.searchsorted(jnp.cumsum(sizes), jnp.arange(rows * top), side="right").astype(jnp.int32)
    listing = labels.reshape(top, rows).T
    listing = listing[jax.random.permutation(jax.random.fold_in(own, 1), rows)]
    turn = jax.random.randint(jax.random.fold_in(own, 2), (rows, 1), 0, top)
    return jnp.take_along_axis(listing, (jnp.arange(top)[None, :] + turn) % top, axis=1)


def portions_of(number_of, total, bound, slope, full):
    weights = [(1 << 20) // math.isqrt(rank ** slope) + 1 for rank in range(1, number_of + 1)]
    largest = bound if full else min(bound, max(-(-total // number_of), total * weights[0] // sum(weights)))
    least = 1 if total - largest >= number_of - 1 else 0
    counts, surplus = [largest] + [least] * (number_of - 1), total - largest - least * (number_of - 1)
    while surplus > 0:
        candidates = [i for i in range(1, number_of) if counts[i] < largest] or [i for i in range(1, number_of) if counts[i] < bound]
        pool, budget = sum([weights[i] for i in candidates]), surplus
        for i in candidates:
            addition = min(bound - counts[i], max(1, budget * weights[i] // pool), surplus)
            counts[i] = counts[i] + addition
            surplus = surplus - addition
    return np.array(counts)


def setup_inputs(seed: int = 0) -> dict:
    splits = jax.random.split(jax.random.key(seed), 7)
    estimate = jnp.clip(jnp.exp(math.log(2.0) - 1.3862944 * jax.random.uniform(splits[0], (ALL_COLUMNS, DEPTH), jnp.float32) ** levels(splits[0], (ALL_COLUMNS, DEPTH), ((0, 8),), -0.2, 0.2)), 0.5, 2.0)
    recorded = jnp.clip(jnp.exp(math.log(4.0) - 2.0794415 * jax.random.uniform(splits[1], (VIEWS, ALL_COLUMNS, DEPTH), jnp.float32) ** levels(splits[1], (VIEWS, ALL_COLUMNS, DEPTH), ((0, 4), (1, 8)), -0.2, 0.2)), 0.5, 4.0)
    resample = draw_resample(jax.random.fold_in(splits[6], 71), 0)
    psf_taps = jnp.clip(jnp.exp(math.log(1.0) - 1.609438 * jax.random.uniform(splits[3], (VIEWS, TAPS), jnp.float32) ** levels(splits[3], (VIEWS, TAPS), ((0, 4),), -0.2, 0.2)), 0.2, 1.0)
    source_brick_keys = jax.random.split(jax.random.fold_in(splits[4], 1), VIEWS * ALL_COLUMNS // COLUMNS)
    source_brick_turns = jax.random.permutation(jax.random.fold_in(splits[4], 3), VIEWS * ALL_COLUMNS // COLUMNS)
    source_brick = jax.vmap(lambda own, number: routed_block(jax.random.fold_in(splits[4], 2), own, number, COLUMNS, BRICKS, SOURCES, CAPACITY, 2))(source_brick_keys, source_brick_turns).reshape((VIEWS, ALL_COLUMNS, SOURCES))
    source_column = set_ends(jax.random.randint(splits[5], (VIEWS, ALL_COLUMNS, SOURCES), 0, COLUMNS), jax.random.fold_in(splits[5], 1), 0, COLUMNS - 1).astype(jnp.int32)
    return dict(estimate=estimate, recorded=recorded, resample=resample, psf_taps=psf_taps, source_brick=source_brick, source_column=source_column)


precise = lax.Precision.HIGHEST


def blur_matrix(taps_row, column_len):
    spread = taps_row / jnp.sum(taps_row)
    tap_count = spread.shape[0]
    half_width = (tap_count - 1) // 2
    row_ids = lax.broadcasted_iota(jnp.int32, (column_len, column_len), 0)
    col_ids = lax.broadcasted_iota(jnp.int32, (column_len, column_len), 1)
    offset = row_ids - col_ids + half_width
    matrix = jnp.zeros((column_len, column_len), spread.dtype)
    for tap_number in range(tap_count):
        matrix = matrix + jnp.where(offset == tap_number, spread[tap_number], jnp.zeros((), spread.dtype))
    return matrix


def reference(estimate, recorded, resample, psf_taps, source_brick, source_column):
    source_ids = (source_brick * COLUMNS + source_column).astype(jnp.int32)
    blurs = [blur_matrix(psf_taps[view], DEPTH) for view in range(VIEWS)]

    def forward(view, field):
        gathered = jnp.zeros(field.shape, field.dtype)
        for branch in range(SOURCES):
            gathered = gathered + jnp.dot(field[source_ids[view, :, branch]], resample[view, branch], precision=precise)
        return jnp.dot(gathered, blurs[view], precision=precise)

    def backward(view, field):
        smeared = jnp.dot(field, blurs[view].T, precision=precise)
        result = jnp.zeros(field.shape, field.dtype)
        for branch in range(SOURCES):
            piece = jnp.dot(smeared, resample[view, branch].T, precision=precise)
            result = result.at[source_ids[view, :, branch]].add(piece)
        return result

    ones_field = jnp.ones(estimate.shape, estimate.dtype)
    normalizer = backward(0, ones_field)
    for view in range(1, VIEWS):
        normalizer = normalizer + backward(view, ones_field)
    for sweep in range(ITERS):
        correction = backward(0, recorded[0] / forward(0, estimate))
        for view in range(1, VIEWS):
            correction = correction + backward(view, recorded[view] / forward(view, estimate))
        estimate = estimate * (correction + 1.0) / (normalizer + 1.0)
    return estimate
```

```python
import functools

import jax
import jax.numpy as jnp
from jax import lax
from jax.experimental import pallas as pl
from jax.experimental.pallas import tpu as pltpu
from jax.sharding import PartitionSpec as P

ITERS = 2
F32 = jnp.float32
BF16 = jnp.bfloat16
VMEM = pltpu.VMEM
MESH = pl.DeviceIdType.MESH


def split(x):
    hi = x.astype(BF16)
    return hi, (x - hi.astype(F32)).astype(BF16)


def dot(a, b):
    return jnp.dot(a, b, preferred_element_type=F32)


def dot3(ah, al, bh, bl):
    return dot(ah, bh) + (dot(ah, bl) + dot(al, bh))


def prep_kernel(taps_ref, r_ref, bh, bl, bth, btl, rh, rl, rth, rtl, unit_ref):
    tap_count = taps_ref.shape[1]
    half = (tap_count - 1) // 2
    depth = bh.shape[0]
    total = taps_ref[0, 0]
    for t in range(1, tap_count):
        total = total + taps_ref[0, t]
    scale = 1.0 / jnp.full((1, depth), total, F32)
    offset = lax.broadcasted_iota(jnp.int32, (depth, depth), 0) - lax.broadcasted_iota(
        jnp.int32, (depth, depth), 1
    ) + half
    blur = jnp.zeros((depth, depth), F32)
    for t in range(tap_count):
        blur = jnp.where(offset == t, taps_ref[0, t], blur)
    blur = blur * scale
    bh[...], bl[...] = split(blur)
    bth[...], btl[...] = split(blur.T)
    smeared = jnp.sum(blur, axis=1, keepdims=True)
    for k in range(r_ref.shape[0]):
        w = r_ref[k]
        rh[k], rl[k] = split(w)
        wt = w.T
        rth[k], rtl[k] = split(wt)
        unit_ref[k : k + 1, :] = jnp.sum(wt * smeared, axis=0, keepdims=True)


def prep(taps, weights):
    sources, depth, _ = weights.shape
    flat = jax.ShapeDtypeStruct((depth, depth), BF16)
    cube = jax.ShapeDtypeStruct((sources, depth, depth), BF16)
    return pl.pallas_call(
        prep_kernel,
        out_shape=[flat] * 4 + [cube] * 4 + [jax.ShapeDtypeStruct((sources, depth), F32)],
        in_specs=[pl.BlockSpec(memory_space=pltpu.SMEM), pl.BlockSpec(memory_space=VMEM)],
        out_specs=[pl.BlockSpec(memory_space=VMEM)] * 9,
        compiler_params=pltpu.CompilerParams(vmem_limit_bytes=40 << 20),
        name="prep",
    )(taps, weights)


def sweep_kernel(
    field, ids_col, ids_row, recorded, bh, bl, bth, btl, rh, rl, rth, rtl, out, gh, gl, ch, cl
):
    total, depth = field.shape
    columns, sources = ids_col.shape
    chunk = min(total, 2048)
    lanes = lax.broadcasted_iota(jnp.int32, (columns, chunk), 1)
    for part in range(total // chunk):
        hi, lo = split(field[part * chunk : (part + 1) * chunk, :])
        for k in range(sources):
            rows = slice(k * columns, (k + 1) * columns)
            pick = jnp.where(ids_col[:, k : k + 1] - part * chunk == lanes, 1.0, 0.0).astype(BF16)
            ph = dot(pick, hi).astype(BF16)
            pm = dot(pick, lo).astype(BF16)
            if part == 0:
                gh[rows, :] = ph
                gl[rows, :] = pm
            else:
                gh[rows, :] = gh[rows, :] + ph
                gl[rows, :] = gl[rows, :] + pm
    forward = jnp.zeros((columns, depth), F32)
    for k in range(sources):
        rows = slice(k * columns, (k + 1) * columns)
        forward = forward + dot3(gh[rows, :], gl[rows, :], rh[k], rl[k])
    fh, fl = split(forward)
    qh, ql = split(recorded[...] / dot3(fh, fl, bh[...], bl[...]))
    sh, sl = split(dot3(qh, ql, bth[...], btl[...]))
    for k in range(sources):
        rows = slice(k * columns, (k + 1) * columns)
        ch[rows, :], cl[rows, :] = split(dot3(sh, sl, rth[k], rtl[k]))
    step = 256
    sub = lax.broadcasted_iota(jnp.int32, (step, columns * sources), 0)

    def scatter(s, carry):
        at = pl.multiple_of(s * step, step)
        put = jnp.where(ids_row[...] - at == sub, 1.0, 0.0).astype(BF16)
        out[pl.ds(at, step), :] = dot(put, ch[...]) + dot(put, cl[...])
        return carry

    lax.fori_loop(0, total // step, scatter, 0)


def run_sweep(field, ids_col, ids_row, recorded, mats):
    total, depth = field.shape
    columns, sources = ids_col.shape
    return pl.pallas_call(
        sweep_kernel,
        out_shape=jax.ShapeDtypeStruct((total, depth), F32),
        in_specs=[pl.BlockSpec(memory_space=VMEM)] * 12,
        out_specs=pl.BlockSpec(memory_space=VMEM),
        scratch_shapes=[pltpu.VMEM((columns * sources, depth), BF16)] * 4,
        compiler_params=pltpu.CompilerParams(vmem_limit_bytes=60 << 20),
        name="sweep",
    )(field, ids_col, ids_row, recorded, *mats)


def gather_stage(mine, field, x, z, v, mate, parity, sizes, sems):
    nx, nz, columns = sizes
    half = columns // 2
    zs, zr, xs, xr, ms, mr, local = sems

    def rows(dx, dz, p):
        brick = lax.rem(x - dx + nx, nx) * nz + lax.rem(z - dz + nz, nz)
        return field.at[pl.ds(pl.multiple_of(brick * columns + p * half, half), half), :]

    keep = pltpu.make_async_copy(mine, rows(0, 0, parity), local)
    keep.start()
    sends = []

    def send(src, dx, dz, s, r, to):
        copy = pltpu.make_async_remote_copy(
            src_ref=src, dst_ref=rows(dx, dz, parity), send_sem=s, recv_sem=r,
            device_id=to, device_id_type=MESH,
        )
        copy.start()
        sends.append(copy)

    def landed(dx, dz, p, s, r, to):
        pltpu.make_async_remote_copy(
            src_ref=mine, dst_ref=rows(dx, dz, p), send_sem=s, recv_sem=r,
            device_id=to, device_id_type=MESH,
        ).wait_recv()

    def to_x(src, dz):
        for dx in range(1, nx):
            send(src, 0, dz, xs.at[dx, dz], xr.at[dx, dz], {"bx": lax.rem(x + dx, nx)})

    to_x(mine, 0)
    for dz in range(nz - 1, 0, -1):
        send(mine, 0, 0, zs.at[dz], zr.at[dz], {"by": lax.rem(z + dz, nz)})
    send(mine, 0, 0, ms.at[0, 0], mr.at[0, 0], {"view": mate})
    for dz in range(1, nz):
        landed(0, dz, parity, zs.at[dz], zr.at[dz], {"by": z})
        to_x(rows(0, dz, parity), dz)
        send(rows(0, dz, parity), 0, dz, ms.at[0, dz], mr.at[0, dz], {"view": mate})
    for dz in range(nz):
        for dx in range(1, nx):
            landed(dx, dz, parity, xs.at[dx, dz], xr.at[dx, dz], {"bx": x})
            send(rows(dx, dz, parity), dx, dz, ms.at[dx, dz], mr.at[dx, dz], {"view": mate})
    for dz in range(nz):
        for dx in range(nx):
            landed(dx, dz, 1 - parity, ms.at[dx, dz], mr.at[dx, dz], {"view": mate})
    for copy in sends:
        copy.wait_send()
    keep.wait()


def scatter_stage(partial, own, x, z, v, mate, parity, sizes, bufs, sems):
    nx, nz, columns = sizes
    half = columns // 2
    nv = lax.axis_size("view")
    mbuf, xbuf, zbuf, ybuf = bufs
    zs, zr, xs, xr, ms, mr, ys, yr = sems

    def rows(dx, dz, p):
        brick = lax.rem(x + dx, nx) * nz + lax.rem(z + dz, nz)
        return pl.ds(pl.multiple_of(brick * columns + p * half, half), half)

    sends = []

    def send(src, dst, s, r, to):
        copy = pltpu.make_async_remote_copy(
            src_ref=src, dst_ref=dst, send_sem=s, recv_sem=r, device_id=to, device_id_type=MESH
        )
        copy.start()
        sends.append(copy)
        return copy

    order_z = list(range(1, nz)) + [0]
    from_mate = {}
    for dx in list(range(1, nx)) + [0]:
        for dz in order_z:
            from_mate[dx, dz] = send(
                partial.at[rows(dx, dz, 1 - parity), :], mbuf.at[dx, dz],
                ms.at[dx, dz], mr.at[dx, dz], {"view": mate},
            )
    from_x = {}
    for dx in range(1, nx):
        for dz in order_z:
            from_mate[dx, dz].wait_recv()
            mbuf[dx, dz] = mbuf[dx, dz] + partial[rows(dx, dz, parity), :]
            from_x[dx, dz] = send(
                mbuf.at[dx, dz], xbuf.at[dx, dz], xs.at[dx, dz], xr.at[dx, dz],
                {"bx": lax.rem(x + dx, nx)},
            )
    from_z = {}
    for dz in order_z:
        from_mate[0, dz].wait_recv()
        acc = mbuf[0, dz] + partial[rows(0, dz, parity), :]
        for dx in range(1, nx):
            from_x[dx, dz].wait_recv()
            acc = acc + xbuf[dx, dz]
        if dz == 0:
            own[...] = acc
        else:
            mbuf[0, dz] = acc
            from_z[dz] = send(
                mbuf.at[0, dz], zbuf.at[dz], zs.at[dz], zr.at[dz], {"by": lax.rem(z + dz, nz)}
            )
    for dz in range(1, nz):
        from_z[dz].wait_recv()
        own[...] = own[...] + zbuf[dz]
    from_y = {}
    for j in range(1, nv // 2):
        from_y[j] = send(
            own, ybuf.at[j], ys.at[j], yr.at[j], {"view": lax.rem(v + 2 * j, nv)}
        )
    total = own[...]
    for j in range(1, nv // 2):
        from_y[j].wait_recv()
        total = total + ybuf[j]
    for copy in sends:
        copy.wait_send()
    return total


def where_am_i():
    nx, nz = lax.axis_size("bx"), lax.axis_size("by")
    x, z, v = lax.axis_index("bx"), lax.axis_index("by"), lax.axis_index("view")
    parity = lax.rem(v, 2)
    return nx, nz, x, z, v, v + 1 - 2 * parity, parity


def greet(nx, nz, x, z, v, mate, with_y):
    barrier = pltpu.get_barrier_semaphore()
    peers = [{"by": lax.rem(z + d, nz)} for d in range(1, nz)]
    peers += [{"bx": lax.rem(x + d, nx)} for d in range(1, nx)]
    peers += [{"view": mate}]
    nv = lax.axis_size("view")
    if with_y:
        peers += [{"view": lax.rem(v + 2 * j, nv)} for j in range(1, nv // 2)]
    for peer in peers:
        pl.semaphore_signal(barrier, inc=1, device_id=peer, device_id_type=MESH)
    pl.semaphore_wait(barrier, len(peers))


def first_kernel(est, field, *sems):
    nx, nz, x, z, v, mate, parity = where_am_i()
    columns = est.shape[0]
    half = columns // 2
    greet(nx, nz, x, z, v, mate, False)
    mine = est.at[pl.ds(pl.multiple_of(parity * half, half), half), :]
    gather_stage(mine, field, x, z, v, mate, parity, (nx, nz, columns), sems)


def update(est, norm, total, parity):
    half = est.shape[0] // 2
    at = pl.ds(pl.multiple_of(parity * half, half), half)
    return est[at, :] * (total + 1.0) / (norm[at, :] + 1.0)


def middle_kernel(partial, est, norm, field, mine, own, *rest):
    nx, nz, x, z, v, mate, parity = where_am_i()
    columns = est.shape[0]
    bufs, sems = rest[:4], rest[4:]
    greet(nx, nz, x, z, v, mate, True)
    sizes = (nx, nz, columns)
    total = scatter_stage(partial, own, x, z, v, mate, parity, sizes, bufs, sems[:8])
    mine[...] = update(est, norm, total, parity)
    gather_stage(mine, field, x, z, v, mate, parity, sizes, sems[8:])


def last_kernel(partial, est, norm, out, own, *rest):
    nx, nz, x, z, v, mate, parity = where_am_i()
    columns = est.shape[0]
    half = columns // 2
    bufs, sems = rest[:4], rest[4:]
    greet(nx, nz, x, z, v, mate, True)
    sizes = (nx, nz, columns)
    total = scatter_stage(partial, own, x, z, v, mate, parity, sizes, bufs, sems[:8])
    at = pl.ds(pl.multiple_of(parity * half, half), half)
    out[at, :] = update(est, norm, total, parity)
    copy = pltpu.make_async_remote_copy(
        src_ref=out.at[at, :], dst_ref=out.at[at, :], send_sem=sems[8], recv_sem=sems[9],
        device_id={"view": mate}, device_id_type=MESH,
    )
    copy.start()
    copy.wait()


def gather_sems(nx, nz):
    dma = pltpu.SemaphoreType.DMA
    return [dma((nz,)), dma((nz,))] + [dma((nx, nz))] * 4 + [dma]


def scatter_scratch(nx, nz, nv, half, depth):
    dma = pltpu.SemaphoreType.DMA
    bufs = [pltpu.VMEM((nx, nz, half, depth), F32)] * 2
    bufs += [pltpu.VMEM((nz, half, depth), F32), pltpu.VMEM((nv // 2, half, depth), F32)]
    return bufs + [dma((nz,)), dma((nz,))] + [dma((nx, nz))] * 4 + [dma((nv // 2,))] * 2


def params(number, vmem=48 << 20):
    return pltpu.CompilerParams(
        collective_id=number, has_side_effects=True, vmem_limit_bytes=vmem
    )


def per_device(estimate, recorded, resample, psf_taps, source_brick, source_column):
    nx, nz, nv = lax.axis_size("bx"), lax.axis_size("by"), lax.axis_size("view")
    columns, depth = estimate.shape
    sources = source_brick.shape[2]
    total = columns * nx * nz
    half = columns // 2
    ids = source_brick[0] * columns + source_column[0]
    ids_turned = ids.T
    ids_row = ids_turned.reshape(1, columns * sources)
    vm, hbm = pl.BlockSpec(memory_space=VMEM), pl.BlockSpec(memory_space=pl.ANY)
    whole = jax.ShapeDtypeStruct((total, depth), F32)
    *mats, unit = prep(psf_taps, resample[0])
    parts = lax.all_gather(ids_turned, ("view", "bx", "by"))
    units = lax.all_gather(unit, "view").reshape(nv * sources, depth)
    field = pl.pallas_call(
        first_kernel,
        out_shape=whole,
        in_specs=[vm],
        out_specs=hbm,
        scratch_shapes=gather_sems(nx, nz),
        compiler_params=params(1),
        name="spread_first",
    )(estimate)
    brick = lax.axis_index("bx") * nz + lax.axis_index("by")
    parts = parts.reshape(nv, nx * nz, sources, columns).transpose(0, 2, 1, 3)
    parts = parts.reshape(nv * sources, total, 1) - brick * columns
    owned = lax.broadcasted_iota(jnp.int32, (1, 1, columns), 2)
    counts = jnp.sum((parts == owned).astype(F32), axis=1)
    norm = jnp.einsum("nc,nd->cd", counts, units, precision=lax.Precision.HIGHEST)
    for turn in range(ITERS):
        partial = run_sweep(field, ids, ids_row, recorded[0], mats)
        scratch = [pltpu.VMEM((half, depth), F32)] + scatter_scratch(nx, nz, nv, half, depth)
        dma = pltpu.SemaphoreType.DMA
        if turn < ITERS - 1:
            field, mine = pl.pallas_call(
                middle_kernel,
                out_shape=[whole, jax.ShapeDtypeStruct((half, depth), F32)],
                in_specs=[vm] * 3,
                out_specs=[hbm, vm],
                scratch_shapes=scratch + gather_sems(nx, nz),
                compiler_params=params(2 + turn),
                name="fold_spread",
            )(partial, estimate, norm)
            estimate = lax.dynamic_slice_in_dim(field, brick * columns, columns, 0)
        else:
            estimate = pl.pallas_call(
                last_kernel,
                out_shape=jax.ShapeDtypeStruct((columns, depth), F32),
                in_specs=[vm] * 3,
                out_specs=vm,
                scratch_shapes=scratch + [dma, dma],
                compiler_params=params(2 + turn),
                name="fold_last",
            )(partial, estimate, norm)
    return estimate


def solution(mesh):
    return jax.shard_map(
        per_device,
        mesh=mesh,
        in_specs=(
            P(("bx", "by"), None),
            P("view", ("bx", "by"), None),
            P("view", None, None, None),
            P("view", None),
            P("view", ("bx", "by"), None),
            P("view", ("bx", "by"), None),
        ),
        out_specs=P(("bx", "by"), None),
        check_vma=False,
    )
```

```python
import jax
import jax.numpy as jnp
from jax import lax
from jax.experimental import pallas as pl
from jax.experimental.pallas import tpu as pltpu
from jax.sharding import PartitionSpec as P

ITERS = 2
F32 = jnp.float32
BF16 = jnp.bfloat16
VMEM = pltpu.VMEM
MESH = pl.DeviceIdType.MESH


def split(x):
    hi = x.astype(BF16)
    return hi, (x - hi.astype(F32)).astype(BF16)


def dot(a, b):
    return jnp.dot(a, b, preferred_element_type=F32)


def dot3(ah, al, bh, bl):
    return dot(ah, bh) + (dot(ah, bl) + dot(al, bh))


def prep_stage(taps_ref, r_ref, bh, bl, bth, btl, rh, rl, rth, rtl, unit):
    tap_count = taps_ref.shape[1]
    half = (tap_count - 1) // 2
    depth = bh.shape[0]
    total = taps_ref[0, 0]
    for t in range(1, tap_count):
        total = total + taps_ref[0, t]
    scale = 1.0 / jnp.full((1, depth), total, F32)
    offset = lax.broadcasted_iota(jnp.int32, (depth, depth), 0) - lax.broadcasted_iota(
        jnp.int32, (depth, depth), 1
    ) + half
    blur = jnp.zeros((depth, depth), F32)
    for t in range(tap_count):
        blur = jnp.where(offset == t, taps_ref[0, t], blur)
    blur = blur * scale
    bh[...], bl[...] = split(blur)
    bth[...], btl[...] = split(blur.T)
    smeared = jnp.sum(blur, axis=1, keepdims=True)
    for k in range(r_ref.shape[0]):
        w = r_ref[k]
        rh[k], rl[k] = split(w)
        wt = w.T
        rth[k], rtl[k] = split(wt)
        unit[k : k + 1, :] = jnp.sum(wt * smeared, axis=0, keepdims=True)


def kernel(
    taps, r_ref, est, recorded, ids_col, ids_row, ids_turned, out, *rest
):
    (
        field, stage, mine, own, my_count, my_unit, norm, partial, mbuf, xbuf, zbuf, ybuf, idsbuf, cnt, units,
        bh, bl, bth, btl, rh, rl, rth, rtl, acc, ch, cl, th, tl, id_cols,
        gz, gx, gm, fz, fx, fm, fy, isem, csem, usem, osem, local,
    ) = rest
    in_vmem = stage.shape[0] == 8
    nx, nz, nv = lax.axis_size("bx"), lax.axis_size("by"), lax.axis_size("view")
    x, z, v = lax.axis_index("bx"), lax.axis_index("by"), lax.axis_index("view")
    parity = lax.rem(v, 2)
    mate = v + 1 - 2 * parity
    columns, depth = est.shape
    half = columns // 2
    sources = ids_col.shape[1]
    pairs = columns * sources

    def peer_x(d):
        return {"bx": lax.rem(x + d, nx)}

    def peer_z(d):
        return {"by": lax.rem(z + d, nz)}

    def peer_v(d):
        return {"view": lax.rem(v + d, nv)}

    def peer_xz(dx, dz):
        return {"bx": lax.rem(x + dx, nx), "by": lax.rem(z + dz, nz)}

    at_half = pl.ds(pl.multiple_of(parity * half, half), half)
    others = [(dx, dz) for dx in range(nx) for dz in range(nz) if dx or dz]
    barrier = pltpu.get_barrier_semaphore()
    peers = [peer_xz(dx, dz) for dx, dz in others] + [peer_v(d) for d in range(1, nv)]
    for peer in peers:
        pl.semaphore_signal(barrier, inc=1, device_id=peer, device_id_type=MESH)
    pl.semaphore_wait(barrier, len(peers))

    def remote(src, dst, sems, at, to):
        return pltpu.make_async_remote_copy(
            src_ref=src, dst_ref=dst, send_sem=sems.at[(0, *at)], recv_sem=sems.at[(1, *at)],
            device_id=to, device_id_type=MESH,
        )

    sends = []

    def send(src, dst, sems, at, to):
        copy = remote(src, dst, sems, at, to)
        copy.start()
        sends.append(copy)
        return copy

    def drain():
        for copy in sends:
            copy.wait_send()
        sends.clear()

    def behind(dx, dz):
        return lax.rem(x - dx + nx, nx) * nz + lax.rem(z - dz + nz, nz)

    def ahead(dx, dz):
        return lax.rem(x + dx, nx) * nz + lax.rem(z + dz, nz)

    def rows(brick, p):
        return pl.ds(pl.multiple_of(brick * columns + p * half, half), half)

    def block(brick):
        return pl.ds(pl.multiple_of(brick * columns, columns), columns)

    lanes = lax.broadcasted_iota(jnp.int32, (columns, columns), 1)

    for k in range(sources):
        id_cols[k] = ids_col[:, k : k + 1]
    acc[...] = jnp.zeros_like(acc)

    def pick_from(value, brick):
        th[...], tl[...] = split(value)

        def one(k, carry):
            at = pl.ds(pl.multiple_of(k * columns, columns), columns)
            pick = jnp.where(id_cols[k] - brick * columns == lanes, 1.0, 0.0).astype(BF16)
            acc[at, :] = acc[at, :] + (dot(pick, th[...]) + dot(pick, tl[...]))
            return carry

        lax.fori_loop(0, sources, one, 0)

    def take(brick):
        if in_vmem:
            pick_from(field[block(brick), :], brick)
        else:
            copy = pltpu.make_async_copy(field.at[block(brick), :], stage, local)
            copy.start()
            copy.wait()
            pick_from(stage[...], brick)

    def forward_stage(turn, between):
        source = est.at[at_half, :] if turn == 0 else mine

        def land(dx, dz, p):
            return field.at[rows(behind(dx, dz), p), :]

        def to_x(src, dz):
            for dx in range(1, nx):
                send(src, land(0, dz, parity), gx, (turn, dx, dz), peer_x(dx))

        def to_mate(src, dx, dz):
            send(src, land(dx, dz, parity), gm, (turn, dx, dz), {"view": mate})

        if turn > 0:
            keep = pltpu.make_async_copy(mine, land(0, 0, parity), local)
            keep.start()
            keep.wait()
            acc[...] = jnp.zeros_like(acc)

        def from_mate(dx, dz):
            remote(
                land(dx, dz, 1 - parity), land(dx, dz, 1 - parity), gm, (turn, dx, dz),
                {"view": mate},
            ).wait_recv()

        to_x(source, 0)
        for dz in range(nz - 1, 0, -1):
            send(source, land(0, 0, parity), gz, (turn, dz), peer_z(dz))
        if turn > 0:
            to_mate(source, 0, 0)
        between()
        here = behind(0, 0)
        if turn == 0:
            pick_from(est[...], here)
        else:
            from_mate(0, 0)
            take(here)
        waiting = []
        for dz in range(1, nz):
            remote(
                land(0, dz, parity), land(0, dz, parity), gz, (turn, dz), peer_z(dz)
            ).wait_recv()
            to_x(land(0, dz, parity), dz)
            to_mate(land(0, dz, parity), 0, dz)
            waiting.append((0, dz))
            if len(waiting) > 1:
                from_mate(*waiting[0])
                take(behind(*waiting.pop(0)))
        for dz in range(nz):
            for dx in range(1, nx):
                remote(
                    land(dx, dz, parity), land(dx, dz, parity), gx, (turn, dx, dz), peer_x(dx)
                ).wait_recv()
                to_mate(land(dx, dz, parity), dx, dz)
                waiting.append((dx, dz))
                from_mate(*waiting[0])
                take(behind(*waiting.pop(0)))
        for at in waiting:
            from_mate(*at)
            take(behind(*at))
        drain()

    def local_stage():
        own_rows = lambda k: pl.ds(pl.multiple_of(k * columns, columns), columns)

        def joined(k, forward):
            gh, gl = split(acc[own_rows(k), :])
            return forward + dot3(gh, gl, rh[k], rl[k])

        forward = lax.fori_loop(0, sources, joined, jnp.zeros((columns, depth), F32))
        fh, fl = split(forward)
        qh, ql = split(recorded[...] / dot3(fh, fl, bh[...], bl[...]))
        th[...], tl[...] = split(dot3(qh, ql, bth[...], btl[...]))

        def piece(k, carry):
            at = own_rows(k)
            ch[at, :], cl[at, :] = split(dot3(th[...], tl[...], rth[k], rtl[k]))
            return carry

        lax.fori_loop(0, sources, piece, 0)

    sub = lax.broadcasted_iota(jnp.int32, (columns, pairs), 0)

    def back_stage(turn, count_copies):
        from_x, from_z = {}, {}

        def produce(dx, dz):
            brick = ahead(dx, dz)
            put = jnp.where(ids_row[...] - brick * columns == sub, 1.0, 0.0).astype(BF16)
            partial[block(brick), :] = dot(put, ch[...]) + dot(put, cl[...])
            return send(
                partial.at[rows(brick, 1 - parity), :], mbuf.at[dx, dz], fm, (turn, dx, dz),
                {"view": mate},
            )

        def pass_on(dx, dz, copy):
            copy.wait_recv()
            total = mbuf[dx, dz] + partial[rows(ahead(dx, dz), parity), :]
            if dx:
                mbuf[dx, dz] = total
                from_x[dx, dz] = send(
                    mbuf.at[dx, dz], xbuf.at[dx, dz], fx, (turn, dx, dz), peer_x(dx)
                )
                return
            for d in range(1, nx):
                from_x[d, dz].wait_recv()
                total = total + xbuf[d, dz]
            if dz:
                mbuf[0, dz] = total
                from_z[dz] = send(mbuf.at[0, dz], zbuf.at[dz], fz, (turn, dz), peer_z(dz))
            else:
                own[...] = total

        order = [(dx, dz) for dx in range(nx - 1, -1, -1) for dz in range(nz - 1, -1, -1)]
        waiting = []
        for dx, dz in order:
            waiting.append((dx, dz, produce(dx, dz)))
            if len(waiting) > 1:
                pass_on(*waiting.pop(0))
        for item in waiting:
            pass_on(*item)
        for dz in range(nz - 1, 0, -1):
            from_z[dz].wait_recv()
            own[...] = own[...] + zbuf[dz]
        from_y = [
            send(own, ybuf.at[turn, j], fy, (turn, j), peer_v(2 * j)) for j in range(1, nv // 2)
        ]
        if turn == 0:
            for copy in count_copies:
                copy.wait_recv()
            summed = jnp.zeros((half, depth), F32)
            for w in range(nv):
                for k in range(sources):
                    summed = summed + cnt[w, at_half, k : k + 1] * units[w, k : k + 1, :]
            norm[...] = summed
        total = own[...]
        for j, copy in enumerate(from_y):
            copy.wait_recv()
            total = total + ybuf[turn, j + 1]
        drain()
        return total

    id_copies = []

    def first_work():
        for dx, dz in others:
            id_copies.append(
                send(ids_turned, idsbuf.at[dx, dz], isem, (dx, dz), peer_xz(dx, dz))
            )
        idsbuf[0, 0] = ids_turned[...]
        prep_stage(taps, r_ref, bh, bl, bth, btl, rh, rl, rth, rtl, my_unit)

    def count_ids():
        for copy in id_copies:
            copy.wait_recv()
        here = behind(0, 0) * columns
        inner = lax.broadcasted_iota(jnp.int32, (columns, columns), 0) + here
        slot = lax.broadcasted_iota(jnp.int32, (columns, 128), 1)
        counted = jnp.zeros((columns, 128), F32)
        for k in range(sources):
            hits = jnp.zeros((columns, columns), F32)
            for dx in range(nx):
                for dz in range(nz):
                    hits = hits + jnp.where(idsbuf[dx, dz, k : k + 1, :] == inner, 1.0, 0.0)
            counted = jnp.where(slot == k, jnp.sum(hits, axis=1, keepdims=True), counted)
        my_count[...] = counted
        cnt[v] = counted
        units[v] = my_unit[...]
        copies = []
        for d in range(1, nv):
            copies.append(send(my_count, cnt.at[v], csem, (d,), peer_v(d)))
            copies.append(send(my_unit, units.at[v], usem, (d,), peer_v(d)))
        return copies

    forward_stage(0, first_work)
    count_copies = count_ids()
    local_stage()
    total = back_stage(0, count_copies)
    for turn in range(1, ITERS):
        now = (est[at_half, :] if turn == 1 else mine[...]) * (total + 1.0) / (norm[...] + 1.0)
        mine[...] = now
        forward_stage(turn, lambda: None)
        local_stage()
        total = back_stage(turn, [])
    here = est[at_half, :] if ITERS == 1 else mine[...]
    out[at_half, :] = here * (total + 1.0) / (norm[...] + 1.0)
    last = remote(out.at[at_half, :], out.at[at_half, :], osem, (0,), {"view": mate})
    last.start()
    last.wait()


def per_device(estimate, recorded, resample, psf_taps, source_brick, source_column):
    nx, nz, nv = lax.axis_size("bx"), lax.axis_size("by"), lax.axis_size("view")
    columns, depth = estimate.shape
    sources = source_brick.shape[2]
    total, half, pairs = columns * nx * nz, columns // 2, columns * sources
    ids = source_brick[0] * columns + source_column[0]
    ids_turned = ids.T
    vm, smem = pl.BlockSpec(memory_space=VMEM), pl.BlockSpec(memory_space=pltpu.SMEM)
    in_vmem = total * depth * 4 <= 8 << 20
    out_shape = [jax.ShapeDtypeStruct((columns, depth), F32)]
    out_specs = [vm]
    scratch = []
    if in_vmem:
        scratch.append(VMEM((total, depth), F32))
    else:
        out_shape.append(jax.ShapeDtypeStruct((total, depth), F32))
        out_specs.append(pl.BlockSpec(memory_space=pl.ANY))
    dma = pltpu.SemaphoreType.DMA
    scratch += [
        VMEM((8 if in_vmem else columns, depth), F32),
        VMEM((half, depth), F32),
        VMEM((half, depth), F32),
        VMEM((columns, 128), F32),
        VMEM((sources, depth), F32),
        VMEM((half, depth), F32),
        VMEM((total, depth), F32),
        VMEM((nx, nz, half, depth), F32),
        VMEM((nx, nz, half, depth), F32),
        VMEM((nz, half, depth), F32),
        VMEM((ITERS, nv // 2, half, depth), F32),
        VMEM((nx, nz, sources, columns), jnp.int32),
        VMEM((nv, columns, 128), F32),
        VMEM((nv, sources, depth), F32),
    ]
    scratch += [VMEM((depth, depth), BF16)] * 4
    scratch += [VMEM((sources, depth, depth), BF16)] * 4
    scratch += [VMEM((pairs, depth), F32)] + [VMEM((pairs, depth), BF16)] * 2
    scratch += [VMEM((columns, depth), BF16)] * 2 + [VMEM((sources, columns, 1), jnp.int32)]
    scratch += [
        dma((2, ITERS, nz)), dma((2, ITERS, nx, nz)), dma((2, ITERS, nx, nz)),
        dma((2, ITERS, nz)), dma((2, ITERS, nx, nz)), dma((2, ITERS, nx, nz)),
        dma((2, ITERS, nv // 2)), dma((2, nx, nz)), dma((2, nv)), dma((2, nv)), dma((2, 1)), dma,
    ]
    return pl.pallas_call(
        kernel,
        out_shape=out_shape,
        in_specs=[smem] + [vm] * 6,
        out_specs=out_specs,
        scratch_shapes=scratch,
        compiler_params=pltpu.CompilerParams(
            collective_id=1, has_side_effects=True, vmem_limit_bytes=(48 if in_vmem else 62) << 20
        ),
        name="deconvolve",
    )(psf_taps, resample[0], estimate, recorded[0], ids, ids_turned.reshape(1, pairs), ids_turned)[0]


def solution(mesh):
    return jax.shard_map(
        per_device,
        mesh=mesh,
        in_specs=(
            P(("bx", "by"), None),
            P("view", ("bx", "by"), None),
            P("view", None, None, None),
            P("view", None),
            P("view", ("bx", "by"), None),
            P("view", ("bx", "by"), None),
        ),
        out_specs=P(("bx", "by"), None),
        check_vma=False,
    )
```

```python
import jax
import jax.numpy as jnp
from jax import lax
from jax.experimental import pallas as pl
from jax.experimental.pallas import tpu as pltpu
from jax.sharding import PartitionSpec as P

ITERS = 2
F32 = jnp.float32
BF16 = jnp.bfloat16
VMEM = pltpu.VMEM
MESH = pl.DeviceIdType.MESH


def split(x):
    hi = x.astype(BF16)
    return hi, (x - hi.astype(F32)).astype(BF16)


def dot(a, b):
    return jnp.dot(a, b, preferred_element_type=F32)


def dot3(ah, al, bh, bl):
    return dot(ah, bh) + (dot(ah, bl) + dot(al, bh))


def prep_stage(taps_ref, r_ref, bh, bl, bth, btl, rh, rl, rth, rtl, unit):
    tap_count = taps_ref.shape[1]
    half = (tap_count - 1) // 2
    depth = bh.shape[0]
    total = taps_ref[0, 0]
    for t in range(1, tap_count):
        total = total + taps_ref[0, t]
    scale = 1.0 / jnp.full((1, depth), total, F32)
    offset = lax.broadcasted_iota(jnp.int32, (depth, depth), 0) - lax.broadcasted_iota(
        jnp.int32, (depth, depth), 1
    ) + half
    blur = jnp.zeros((depth, depth), F32)
    for t in range(tap_count):
        blur = jnp.where(offset == t, taps_ref[0, t], blur)
    blur = blur * scale
    bh[...], bl[...] = split(blur)
    bth[...], btl[...] = split(blur.T)
    smeared = jnp.sum(blur, axis=1, keepdims=True)
    for k in range(r_ref.shape[0]):
        w = r_ref[k]
        rh[k], rl[k] = split(w)
        wt = w.T
        rth[k], rtl[k] = split(wt)
        unit[k : k + 1, :] = jnp.sum(wt * smeared, axis=0, keepdims=True)


def kernel(
    taps, r_ref, est, recorded, ids_col, ids_row, ids_turned, out, *rest
):
    (
        field, stage, mine, own, my_count, my_unit, norm, partial, mbuf, xbuf, zbuf, ybuf, idsbuf, cnt, units,
        bh, bl, bth, btl, rh, rl, rth, rtl, acc, ch, cl, th, tl, id_cols,
        gz, gx, gm, fz, fx, fm, fy, isem, csem, usem, osem, local,
    ) = rest
    in_vmem = stage.shape[0] == 8
    nx, nz, nv = lax.axis_size("bx"), lax.axis_size("by"), lax.axis_size("view")
    x, z, v = lax.axis_index("bx"), lax.axis_index("by"), lax.axis_index("view")
    parity = lax.rem(v, 2)
    mate = v + 1 - 2 * parity
    columns, depth = est.shape
    half = columns // 2
    sources = ids_col.shape[1]
    pairs = columns * sources

    def peer_x(d):
        return {"bx": lax.rem(x + d, nx)}

    def peer_z(d):
        return {"by": lax.rem(z + d, nz)}

    def peer_v(d):
        return {"view": lax.rem(v + d, nv)}

    def peer_xz(dx, dz):
        return {"bx": lax.rem(x + dx, nx), "by": lax.rem(z + dz, nz)}

    at_half = pl.ds(pl.multiple_of(parity * half, half), half)
    others = [(dx, dz) for dx in range(nx) for dz in range(nz) if dx or dz]
    barrier = pltpu.get_barrier_semaphore()
    peers = [peer_xz(dx, dz) for dx, dz in others] + [peer_v(d) for d in range(1, nv)]
    for peer in peers:
        pl.semaphore_signal(barrier, inc=1, device_id=peer, device_id_type=MESH)
    pl.semaphore_wait(barrier, len(peers))

    def remote(src, dst, sems, at, to):
        return pltpu.make_async_remote_copy(
            src_ref=src, dst_ref=dst, send_sem=sems.at[(0, *at)], recv_sem=sems.at[(1, *at)],
            device_id=to, device_id_type=MESH,
        )

    sends = []

    def send(src, dst, sems, at, to):
        copy = remote(src, dst, sems, at, to)
        copy.start()
        sends.append(copy)
        return copy

    def drain():
        for copy in sends:
            copy.wait_send()
        sends.clear()

    def behind(dx, dz):
        return lax.rem(x - dx + nx, nx) * nz + lax.rem(z - dz + nz, nz)

    def ahead(dx, dz):
        return lax.rem(x + dx, nx) * nz + lax.rem(z + dz, nz)

    def rows(brick, p):
        return pl.ds(pl.multiple_of(brick * columns + p * half, half), half)

    def block(brick):
        return pl.ds(pl.multiple_of(brick * columns, columns), columns)

    lanes = lax.broadcasted_iota(jnp.int32, (columns, columns), 1)

    for k in range(sources):
        id_cols[k] = ids_col[:, k : k + 1]
    acc[...] = jnp.zeros_like(acc)

    def pick_from(value, brick):
        th[...], tl[...] = split(value)

        def one(k, carry):
            at = pl.ds(pl.multiple_of(k * columns, columns), columns)
            pick = jnp.where(id_cols[k] - brick * columns == lanes, 1.0, 0.0).astype(BF16)
            acc[at, :] = acc[at, :] + (dot(pick, th[...]) + dot(pick, tl[...]))
            return carry

        lax.fori_loop(0, sources, one, 0)

    def take(brick):
        if in_vmem:
            pick_from(field[block(brick), :], brick)
        else:
            copy = pltpu.make_async_copy(field.at[block(brick), :], stage, local)
            copy.start()
            copy.wait()
            pick_from(stage[...], brick)

    def forward_stage(turn, between):
        source = est.at[at_half, :] if turn == 0 else mine

        def land(dx, dz, p):
            return field.at[rows(behind(dx, dz), p), :]

        def to_x(src, dz):
            for dx in range(1, nx):
                send(src, land(0, dz, parity), gx, (turn, dx, dz), peer_x(dx))

        def to_mate(src, dx, dz):
            send(src, land(dx, dz, parity), gm, (turn, dx, dz), {"view": mate})

        if turn > 0:
            keep = pltpu.make_async_copy(mine, land(0, 0, parity), local)
            keep.start()
            keep.wait()
            acc[...] = jnp.zeros_like(acc)

        def from_mate(dx, dz):
            remote(
                land(dx, dz, 1 - parity), land(dx, dz, 1 - parity), gm, (turn, dx, dz),
                {"view": mate},
            ).wait_recv()

        to_x(source, 0)
        steps = sorted(range(1, nz), key=lambda d: min(d, nz - d))

        def to_z(dz):
            send(source, land(0, 0, parity), gz, (turn, dz), peer_z(dz))

        if nz > 1:
            to_z(steps[0])
        if turn > 0:
            to_mate(source, 0, 0)
        between()
        here = behind(0, 0)
        if turn == 0:
            pick_from(est[...], here)
        else:
            from_mate(0, 0)
            take(here)
        waiting = []
        for number, dz in enumerate(steps):
            remote(
                land(0, dz, parity), land(0, dz, parity), gz, (turn, dz), peer_z(dz)
            ).wait_recv()
            if number + 1 < len(steps):
                to_z(steps[number + 1])
            to_x(land(0, dz, parity), dz)
            to_mate(land(0, dz, parity), 0, dz)
            waiting.append((0, dz))
            if len(waiting) > 1:
                from_mate(*waiting[0])
                take(behind(*waiting.pop(0)))
        for dz in [0] + steps:
            for dx in range(1, nx):
                remote(
                    land(dx, dz, parity), land(dx, dz, parity), gx, (turn, dx, dz), peer_x(dx)
                ).wait_recv()
                to_mate(land(dx, dz, parity), dx, dz)
                waiting.append((dx, dz))
                from_mate(*waiting[0])
                take(behind(*waiting.pop(0)))
        for at in waiting:
            from_mate(*at)
            take(behind(*at))
        drain()

    def local_stage():
        own_rows = lambda k: pl.ds(pl.multiple_of(k * columns, columns), columns)

        def joined(k, forward):
            gh, gl = split(acc[own_rows(k), :])
            return forward + dot3(gh, gl, rh[k], rl[k])

        forward = lax.fori_loop(0, sources, joined, jnp.zeros((columns, depth), F32))
        fh, fl = split(forward)
        qh, ql = split(recorded[...] / dot3(fh, fl, bh[...], bl[...]))
        th[...], tl[...] = split(dot3(qh, ql, bth[...], btl[...]))

        def piece(k, carry):
            at = own_rows(k)
            ch[at, :], cl[at, :] = split(dot3(th[...], tl[...], rth[k], rtl[k]))
            return carry

        lax.fori_loop(0, sources, piece, 0)

    sub = lax.broadcasted_iota(jnp.int32, (columns, pairs), 0)

    def back_stage(turn, count_copies):
        from_x, from_z = {}, {}

        def produce(dx, dz):
            brick = ahead(dx, dz)
            put = jnp.where(ids_row[...] - brick * columns == sub, 1.0, 0.0).astype(BF16)
            partial[block(brick), :] = dot(put, ch[...]) + dot(put, cl[...])
            return send(
                partial.at[rows(brick, 1 - parity), :], mbuf.at[dx, dz], fm, (turn, dx, dz),
                {"view": mate},
            )

        def pass_on(dx, dz, copy):
            copy.wait_recv()
            total = mbuf[dx, dz] + partial[rows(ahead(dx, dz), parity), :]
            if dx:
                mbuf[dx, dz] = total
                from_x[dx, dz] = send(
                    mbuf.at[dx, dz], xbuf.at[dx, dz], fx, (turn, dx, dz), peer_x(dx)
                )
                return
            for d in range(1, nx):
                from_x[d, dz].wait_recv()
                total = total + xbuf[d, dz]
            if dz:
                mbuf[0, dz] = total
                from_z[dz] = send(mbuf.at[0, dz], zbuf.at[dz], fz, (turn, dz), peer_z(dz))
            else:
                own[...] = total

        order = []
        for dz in range(nz - 1, -1, -1):
            order += [(dx, dz) for dx in range(nx - 1, 0, -1)]
            if dz + 1 < nz:
                order.append((0, dz + 1))
        order.append((0, 0))
        waiting = []
        for dx, dz in order:
            waiting.append((dx, dz, produce(dx, dz)))
            if len(waiting) > 1:
                pass_on(*waiting.pop(0))
        for item in waiting:
            pass_on(*item)
        for dz in range(nz - 1, 0, -1):
            from_z[dz].wait_recv()
            own[...] = own[...] + zbuf[dz]
        from_y = [
            send(own, ybuf.at[turn, j], fy, (turn, j), peer_v(2 * j)) for j in range(1, nv // 2)
        ]
        if turn == 0:
            for copy in count_copies:
                copy.wait_recv()
            summed = jnp.zeros((half, depth), F32)
            for w in range(nv):
                for k in range(sources):
                    summed = summed + cnt[w, at_half, k : k + 1] * units[w, k : k + 1, :]
            norm[...] = summed
        total = own[...]
        for j, copy in enumerate(from_y):
            copy.wait_recv()
            total = total + ybuf[turn, j + 1]
        drain()
        return total

    id_copies = []

    def first_work():
        for dx, dz in others:
            id_copies.append(
                send(ids_turned, idsbuf.at[dx, dz], isem, (dx, dz), peer_xz(dx, dz))
            )
        idsbuf[0, 0] = ids_turned[...]
        prep_stage(taps, r_ref, bh, bl, bth, btl, rh, rl, rth, rtl, my_unit)

    def count_ids():
        for copy in id_copies:
            copy.wait_recv()
        here = behind(0, 0) * columns
        inner = lax.broadcasted_iota(jnp.int32, (columns, columns), 0) + here
        slot = lax.broadcasted_iota(jnp.int32, (columns, 128), 1)
        counted = jnp.zeros((columns, 128), F32)
        for k in range(sources):
            hits = jnp.zeros((columns, columns), F32)
            for dx in range(nx):
                for dz in range(nz):
                    hits = hits + jnp.where(idsbuf[dx, dz, k : k + 1, :] == inner, 1.0, 0.0)
            counted = jnp.where(slot == k, jnp.sum(hits, axis=1, keepdims=True), counted)
        my_count[...] = counted
        cnt[v] = counted
        units[v] = my_unit[...]
        copies = []
        for d in range(1, nv):
            copies.append(send(my_count, cnt.at[v], csem, (d,), peer_v(d)))
            copies.append(send(my_unit, units.at[v], usem, (d,), peer_v(d)))
        return copies

    forward_stage(0, first_work)
    count_copies = count_ids()
    local_stage()
    total = back_stage(0, count_copies)
    for turn in range(1, ITERS):
        now = (est[at_half, :] if turn == 1 else mine[...]) * (total + 1.0) / (norm[...] + 1.0)
        mine[...] = now
        forward_stage(turn, lambda: None)
        local_stage()
        total = back_stage(turn, [])
    here = est[at_half, :] if ITERS == 1 else mine[...]
    out[at_half, :] = here * (total + 1.0) / (norm[...] + 1.0)
    last = remote(out.at[at_half, :], out.at[at_half, :], osem, (0,), {"view": mate})
    last.start()
    last.wait()


def per_device(estimate, recorded, resample, psf_taps, source_brick, source_column):
    nx, nz, nv = lax.axis_size("bx"), lax.axis_size("by"), lax.axis_size("view")
    columns, depth = estimate.shape
    sources = source_brick.shape[2]
    total, half, pairs = columns * nx * nz, columns // 2, columns * sources
    ids = source_brick[0] * columns + source_column[0]
    ids_turned = ids.T
    vm, smem = pl.BlockSpec(memory_space=VMEM), pl.BlockSpec(memory_space=pltpu.SMEM)
    in_vmem = total * depth * 4 <= 8 << 20
    out_shape = [jax.ShapeDtypeStruct((columns, depth), F32)]
    out_specs = [vm]
    scratch = []
    if in_vmem:
        scratch.append(VMEM((total, depth), F32))
    else:
        out_shape.append(jax.ShapeDtypeStruct((total, depth), F32))
        out_specs.append(pl.BlockSpec(memory_space=pl.ANY))
    dma = pltpu.SemaphoreType.DMA
    scratch += [
        VMEM((8 if in_vmem else columns, depth), F32),
        VMEM((half, depth), F32),
        VMEM((half, depth), F32),
        VMEM((columns, 128), F32),
        VMEM((sources, depth), F32),
        VMEM((half, depth), F32),
        VMEM((total, depth), F32),
        VMEM((nx, nz, half, depth), F32),
        VMEM((nx, nz, half, depth), F32),
        VMEM((nz, half, depth), F32),
        VMEM((ITERS, nv // 2, half, depth), F32),
        VMEM((nx, nz, sources, columns), jnp.int32),
        VMEM((nv, columns, 128), F32),
        VMEM((nv, sources, depth), F32),
    ]
    scratch += [VMEM((depth, depth), BF16)] * 4
    scratch += [VMEM((sources, depth, depth), BF16)] * 4
    scratch += [VMEM((pairs, depth), F32)] + [VMEM((pairs, depth), BF16)] * 2
    scratch += [VMEM((columns, depth), BF16)] * 2 + [VMEM((sources, columns, 1), jnp.int32)]
    scratch += [
        dma((2, ITERS, nz)), dma((2, ITERS, nx, nz)), dma((2, ITERS, nx, nz)),
        dma((2, ITERS, nz)), dma((2, ITERS, nx, nz)), dma((2, ITERS, nx, nz)),
        dma((2, ITERS, nv // 2)), dma((2, nx, nz)), dma((2, nv)), dma((2, nv)), dma((2, 1)), dma,
    ]
    return pl.pallas_call(
        kernel,
        out_shape=out_shape,
        in_specs=[smem] + [vm] * 6,
        out_specs=out_specs,
        scratch_shapes=scratch,
        compiler_params=pltpu.CompilerParams(
            collective_id=1, has_side_effects=True, vmem_limit_bytes=(48 if in_vmem else 62) << 20
        ),
        name="deconvolve",
    )(psf_taps, resample[0], estimate, recorded[0], ids, ids_turned.reshape(1, pairs), ids_turned)[0]


def solution(mesh):
    return jax.shard_map(
        per_device,
        mesh=mesh,
        in_specs=(
            P(("bx", "by"), None),
            P("view", ("bx", "by"), None),
            P("view", None, None, None),
            P("view", None),
            P("view", ("bx", "by"), None),
            P("view", ("bx", "by"), None),
        ),
        out_specs=P(("bx", "by"), None),
        check_vma=False,
    )
```
